512 devices in a mesh: segment: 16 (over x, y), node: 32 (over z, core).
Axes of the slice: x: 4, y: 4, z: 16, core: 2. Of those that a mesh axis runs over, the one named last changes fastest.
Arguments:
- activations: bfloat16 [16, 8192, 512], P('segment', 'node'), may hold values from -8 to 8
- norm_gain: float32 [16, 512], P('segment'), may hold values from 0.5 to 1.5
- project_in: bfloat16 [16, 512, 1536], P('segment'), may hold values from -0.25 to 0.25
- project_out: bfloat16 [16, 512, 512], P('segment'), may hold values from -0.5 to 0.5
- virtual_keys: bfloat16 [16, 4, 512], P('segment'), may hold values from -6 to 6
- virtual_id: int32 [8192, 1], P('node'), may hold values from 0 to 3
- local_rows: int32 [16, 8192], P(None, 'node'), may hold values from 0 to 127
- slot_block: int32 [64, 8], P('node'), may hold values from 0 to 63, as said below
- slot_count: int32 [64], P('node'), may hold values from 1 to 8, as said below
- slot_rows: int32 [64, 8, 4, 128], P('node'), may hold values from 0 to 127
Outputs:
- handed: bfloat16 [16, 8192, 512], P('segment', 'node')
The draws below stay inside these ranges and needn't reach their ends.
Inputs may be any that keep to these rules, and one draw needn't show every extreme that they name: `virtual_id`: every virtual node has a member. `slot_block`: blocks d * 2 to (d + 1) * 2 - 1 lie on device d of node; every entry names a block of another device than the destination block's, and all entries of one device's rows that name blocks of the same device name the same block. `slot_count`: some block has 8 live slots.
All inputs are finite; a program needn't handle non-finite values.
Results may differ from the reference program's by a relative error of at most 0.0065.
Values may be sent and summed in bfloat16 or wider, within the bound.
A program may use at most 64 MiB of HBM per device.

```python
import jax
import jax.numpy as jnp
from jax import lax

D = 512
HEADS = 8
HDIM = 64
VN = 4
BLK = 128
BLK_DEV = 2
EX = 8
KL = 16
KE = 4
GROUP = 32
LAYERS = 16
NODES = 8192
NBLK = 64


def draw_activations(key, part):
    noise_key, mean_key = jax.random.split(key, 2)
    common = jax.random.normal(mean_key, (LAYERS, 1, D), jnp.float32)
    position = jnp.arange(NODES, dtype=jnp.float32) / NODES
    noise = jax.random.normal(noise_key, (LAYERS, NODES, D), jnp.float32)
    ramp = 0.5 + position
    field = noise + ramp[None, :, None] * common
    return jnp.clip(field, -8.0, 8.0).astype(jnp.bfloat16)


def draw_slot_block(key, part):
    offset_key, block_key = jax.random.split(jax.random.fold_in(key, 11))
    offsets = jax.random.randint(offset_key, (GROUP,), 0, GROUP - 1)
    wanted = jax.random.randint(block_key, (GROUP, GROUP), 0, BLK_DEV)
    block_ids = jnp.arange(NBLK, dtype=jnp.int32)
    owner = block_ids // BLK_DEV
    slot_ids = (block_ids % BLK_DEV)[:, None] * EX + jnp.arange(EX, dtype=jnp.int32)[None, :]
    stepped = (slot_ids + offsets[owner][:, None]) % (GROUP - 1)
    peer = (owner[:, None] + 1 + stepped) % GROUP
    return (peer * BLK_DEV + wanted[owner[:, None], peer]).astype(jnp.int32)


def draw_slot_count(key, part):
    level_key, count_key, pick_key = jax.random.split(jax.random.fold_in(key, 23), 3)
    levels = jax.random.randint(level_key, (GROUP,), 0, 4)
    picked = jax.random.randint(pick_key, (), 0, GROUP)
    levels = jnp.where(jnp.arange(GROUP, dtype=jnp.int32) == picked, 3, levels)
    owner = jnp.arange(NBLK, dtype=jnp.int32) // BLK_DEV
    reach = jnp.minimum(EX, jnp.left_shift(1, levels[owner]))
    counts = 1 + jax.random.randint(count_key, (NBLK,), 0, reach)
    first = jnp.arange(NBLK, dtype=jnp.int32) == picked * BLK_DEV
    return jnp.where(first, EX, jnp.minimum(counts, EX)).astype(jnp.int32)


def place_ends(entries, stream_key, least, top_value):
    longest = entries.shape.index(max(entries.shape))
    spots = []
    for shift in (0, 1):
        where = [jax.random.randint(jax.random.fold_in(stream_key, axis), (), 0, length) for axis, length in enumerate(entries.shape)]
        where[longest] = (where[longest] + shift) % entries.shape[longest]
        spots.append(tuple(where))
    return entries.at[spots[0]].set(least).at[spots[1]].set(top_value)


def shard_levels(stream_key, extent, cuts, smallest, top_value):
    def one(axis_at, shards_of):
        steps = jax.random.uniform(jax.random.fold_in(jax.random.fold_in(stream_key, 6), axis_at), (shards_of,), jnp.float32, smallest / len(cuts), top_value / len(cuts))
        return jnp.repeat(jnp.exp(steps), extent[axis_at] // shards_of).reshape((-1,) + (1,) * (len(extent) - axis_at - 1))

    level = one(*cuts[0])
    for cut in cuts[1:]:
        level = level * one(*cut)
    return level


def distinct(key, rows, count, top, lift):
    order = jax.random.permutation(jax.random.fold_in(key, 1), count)
    favour = order
    for power in range(3):
        favour = favour * favour // count
    favour = favour * lift // count
    chance = jax.random.randint(jax.random.fold_in(key, 2), (rows, count), 0, 4096) + favour
    sure = jax.random.permutation(jax.random.fold_in(key, 3), rows)[jnp.arange(count) % rows]
    chance = jnp.where(jnp.arange(rows)[:, None] == sure[None, :], 1 << 14, chance)
    priority = chance * count + jnp.arange(count)
    return lax.top_k(priority.astype(jnp.int32), top)[1].astype(jnp.int32)


def centred(stream_key, shape, scale, bound, shards=(), kind=jnp.bfloat16):
    array = scale * jax.random.normal(stream_key, shape, jnp.float32)
    if shards:
        array = array * shard_levels(stream_key, shape, shards, -0.22, 0.18)
    return jnp.clip(array, -bound, bound).astype(kind)


def setup_inputs(seed: int = 0) -> dict:
    key_list = jax.random.split(jax.random.key(seed), 11)
    activations = draw_activations(jax.random.fold_in(key_list[10], 71), 0)
    norm_gain = jnp.clip(1.0 + 0.1 * jax.random.normal(key_list[1], (LAYERS, D), jnp.float32), 0.5, 1.5)
    project_in = centred(key_list[2], (LAYERS, D, 3 * D), D ** -0.5, 0.25, ((0, 16),))
    project_out = centred(key_list[3], (LAYERS, D, D), (D // 4) ** -0.5, 0.5, ((0, 16),))
    virtual_keys = centred(key_list[4], (LAYERS, VN, D), 1.0, 6.0, ((0, 16),))
    virtual_id = distinct(key_list[5], NODES, VN, 1, 0)
    local_rows = place_ends(jax.random.randint(key_list[6], (KL, NODES), 0, BLK), jax.random.fold_in(key_list[6], 1), 0, BLK - 1).astype(jnp.int32)
    slot_block = draw_slot_block(jax.random.fold_in(key_list[10], 71), 0)
    slot_count = draw_slot_count(jax.random.fold_in(key_list[10], 71), 0)
    slot_rows = place_ends(jax.random.randint(key_list[9], (NBLK, EX, KE, BLK), 0, BLK), jax.random.fold_in(key_list[9], 1), 0, BLK - 1).astype(jnp.int32)
    return {"activations": activations, "norm_gain": norm_gain, "project_in": project_in, "project_out": project_out, "virtual_keys": virtual_keys, "virtual_id": virtual_id, "local_rows": local_rows, "slot_block": slot_block, "slot_count": slot_count, "slot_rows": slot_rows}


cap_limit = 10.0
epsilon = 1e-05

def capped(raw_score):
    return cap_limit * jnp.tanh(raw_score / cap_limit)

def layer_norm(rows_in, gain_row):
    widened = rows_in.astype(jnp.float32)
    center = widened - lax.optimization_barrier(jnp.mean(widened, axis=-1, keepdims=True))
    spread = lax.optimization_barrier(jnp.mean(center * center, axis=-1, keepdims=True))
    return (center * lax.rsqrt(spread + epsilon) * gain_row).astype(jnp.bfloat16)

def edge_counts(index_rows):
    columns = jnp.arange(BLK, dtype=jnp.int32)
    return lax.optimization_barrier(jnp.sum((index_rows.astype(jnp.int32)[..., None] == columns).astype(jnp.float32), axis=0))

def pair_single(query_rows, key_rows, value_rows, counts):
    shaped = (BLK, HEADS, HDIM)
    query_wide = query_rows.astype(jnp.float32).reshape(shaped)
    key_wide = key_rows.astype(jnp.float32).reshape(shaped)
    value_wide = value_rows.astype(jnp.float32).reshape(shaped)
    raw_score = jnp.einsum('qhd,khd->hqk', query_wide, key_wide) * HDIM ** (-0.5)
    weights = (counts[None] * jnp.exp(capped(raw_score))).astype(jnp.bfloat16)
    numerator = jnp.einsum('hqk,khd->qhd', weights.astype(jnp.float32), value_wide)
    denominator = lax.optimization_barrier(jnp.sum(weights.astype(jnp.float32), axis=2)).T
    return (numerator, denominator)

def reference(activations, norm_gain, project_in, project_out, virtual_keys, virtual_id, local_rows, slot_block, slot_count, slot_rows):
    member = (virtual_id[:, 0].astype(jnp.int32)[:, None] == jnp.arange(VN, dtype=jnp.int32)[None, :]).astype(jnp.float32)
    block_list = jnp.arange(NBLK, dtype=jnp.int32)
    slot_list = jnp.arange(EX, dtype=jnp.int32)

    def one_layer(layer_index):
        normed = layer_norm(activations[layer_index], norm_gain[layer_index])
        projected = jnp.dot(normed, project_in[layer_index], preferred_element_type=jnp.float32)
        queries = projected[:, :D].astype(jnp.bfloat16)
        keys_all = projected[:, D:2 * D].astype(jnp.bfloat16)
        values_all = projected[:, 2 * D:].astype(jnp.bfloat16)
        own_key = jnp.dot(member, virtual_keys[layer_index].astype(jnp.float32), precision=lax.Precision.HIGHEST)
        pool_raw = lax.optimization_barrier(jnp.sum((own_key * keys_all.astype(jnp.float32)).reshape(NODES, HEADS, HDIM), axis=2)) * HDIM ** (-0.5)
        pool_weight = jnp.exp(capped(pool_raw)).astype(jnp.bfloat16)
        weighted = pool_weight.astype(jnp.float32)[:, :, None] * values_all.astype(jnp.float32).reshape(NODES, HEADS, HDIM)
        pool_num = jnp.einsum('rj,rhd->jhd', member, weighted, precision=lax.Precision.HIGHEST)
        pool_den = jnp.dot(member.T, pool_weight.astype(jnp.float32), precision=lax.Precision.HIGHEST)
        pooled = pool_num / pool_den[:, :, None]

        def one_block(block_index):
            start = (block_index * BLK).astype(jnp.int32)
            query_rows = lax.dynamic_slice_in_dim(queries, start, BLK, 0)
            key_rows = lax.dynamic_slice_in_dim(keys_all, start, BLK, 0)
            value_rows = lax.dynamic_slice_in_dim(values_all, start, BLK, 0)
            local_index = lax.dynamic_slice_in_dim(local_rows, start, BLK, 1)
            numerator, denominator = pair_single(query_rows, key_rows, value_rows, edge_counts(local_index))

            def add_slot(running, slot_index):
                source = (slot_block[block_index, slot_index] * BLK).astype(jnp.int32)
                live_flag = (slot_index < slot_count[block_index]).astype(jnp.float32)
                counts_now = edge_counts(slot_rows[block_index, slot_index]) * live_flag
                extra_num, extra_den = pair_single(query_rows, lax.dynamic_slice_in_dim(keys_all, source, BLK, 0), lax.dynamic_slice_in_dim(values_all, source, BLK, 0), counts_now)
                return ((running[0] + extra_num, running[1] + extra_den), None)
            (numerator, denominator), _ = lax.scan(add_slot, (numerator, denominator), slot_list)
            return numerator / denominator[:, :, None]
        attended = lax.map(one_block, block_list).reshape(NODES, D)
        broadcast_pool = jnp.dot(member, pooled.reshape(VN, D), precision=lax.Precision.HIGHEST)
        mixed = (attended + broadcast_pool).astype(jnp.bfloat16)
        return (activations[layer_index].astype(jnp.float32) + jnp.dot(mixed, project_out[layer_index], preferred_element_type=jnp.float32)).astype(jnp.bfloat16)
    layers_out = lax.map(one_layer, jnp.arange(LAYERS, dtype=jnp.int32))
    return jnp.roll(layers_out, 1, axis=0)
```

```python
import functools
import math

import jax
import jax.numpy as jnp
from jax import lax
from jax.experimental import pallas as pl
from jax.experimental.pallas import tpu as pltpu
from jax.sharding import PartitionSpec as P

HEADS = 8
LANES = 128
CAP = 10.0
EPSILON = 1e-05
MESH = pl.DeviceIdType.MESH


def normalize(wide, gain):
    center = wide - jnp.mean(wide, axis=-1, keepdims=True)
    spread = jnp.mean(center * center, axis=-1, keepdims=True)
    return (center * lax.rsqrt(spread + EPSILON) * gain).astype(jnp.bfloat16)


def weight_of(raw, head_width):
    inner = jnp.tanh(raw * (head_width**-0.5 / CAP))
    return jnp.exp2(inner * (CAP * math.log2(math.e)))


def layer_kernel(
    sizes,
    x_hbm,
    gain_ref,
    win_hbm,
    wout_hbm,
    vkey_ref,
    vid_ref,
    local_ref,
    block_ref,
    live_ref,
    rows_ref,
    out_hbm,
    x_own,
    w_in,
    w_out,
    queries,
    own_kv,
    ring,
    near,
    counts,
    acc,
    vid_wide,
    pool,
    pool_ring,
    pool_sum,
    pool_near,
    stage,
    load_sem,
    main_send,
    near_send,
    ring_recv,
    own_sem,
    pool_send,
    pool_recv,
    pool_sem,
    out_send,
    out_recv,
):
    chips, sections, block, width, slots, slot_edges, local_edges, virtuals = sizes
    rows = 2 * block
    head_width = width // HEADS
    slabs = width // LANES
    half = chips // 2
    chunks = chips - 1
    last = chunks - 1
    me = lax.axis_index("node")
    section = lax.axis_index("segment")
    chip = me // 2
    core = me % 2
    right = (me + 2) % (2 * chips)
    left = (me + 2 * chips - 2) % (2 * chips)
    partner = chip * 2 + (1 - core)
    following = (section + 1) % sections
    previous = (section + sections - 1) % sections

    def remote(source, target, send, recv, device):
        return pltpu.make_async_remote_copy(
            src_ref=source,
            dst_ref=target,
            send_sem=send,
            recv_sem=recv,
            device_id=device,
            device_id_type=MESH,
        )

    beside = ({"node": right}, {"node": left})

    def onward(side, source, to):
        return remote(
            source, ring.at[side, to], main_send.at[side, to], ring_recv.at[side, to], beside[side]
        )

    def across(side, at):
        return remote(
            ring.at[side, at],
            ring.at[2 + side, at],
            near_send.at[side, at],
            ring_recv.at[2 + side, at],
            {"node": partner},
        )

    def arrived(lane, at):
        remote(
            ring.at[lane, at],
            ring.at[lane, at],
            near_send.at[0, 0],
            ring_recv.at[lane, at],
            {"node": partner},
        ).wait_recv()

    def pool_onward(side, source, to):
        return remote(
            source, pool_ring.at[side, to], pool_send.at[side, to], pool_recv.at[side, to], beside[side]
        )

    barrier = pltpu.get_barrier_semaphore()
    for device in (
        {"node": right},
        {"node": left},
        {"node": partner},
        {"segment": following},
        {"segment": previous},
    ):
        pl.semaphore_signal(barrier, inc=1, device_id=device, device_id_type=MESH)
    pl.semaphore_wait(barrier, 5)

    for part in range(2):
        for side in range(2):
            onward(side, x_hbm.at[pl.ds(part * block, block)], part).start()
    own_out = remote(x_hbm, near, own_sem.at[0], own_sem.at[1], {"node": partner})
    own_out.start()
    load_x = pltpu.make_async_copy(x_hbm, x_own, load_sem.at[0])
    load_in = pltpu.make_async_copy(win_hbm, w_in, load_sem.at[1])
    load_out = pltpu.make_async_copy(wout_hbm, w_out, load_sem.at[2])
    load_x.start()
    load_in.start()
    load_out.start()

    lane = lax.broadcasted_iota(jnp.int32, (block, LANES), 1)
    low_f = jnp.where(lane < head_width, 1.0, 0.0).astype(jnp.float32)
    high_f = 1.0 - low_f
    low = low_f.astype(jnp.bfloat16)
    high = high_f.astype(jnp.bfloat16)
    gain = gain_ref[...]

    def attend(kv, tally):
        doubled = jnp.concatenate([tally, tally], axis=1)
        for slab in range(slabs):
            at = slab * LANES
            keys = kv[:, at : at + LANES]
            values = kv[:, width + at : width + at + LANES]
            key_pair = jnp.concatenate([keys * low, keys * high], axis=0)
            raw = lax.dot_general(
                queries[:, at : at + LANES],
                key_pair,
                (((1,), (1,)), ((), ())),
                preferred_element_type=jnp.float32,
            )
            weights = (doubled * weight_of(raw, head_width)).astype(jnp.bfloat16)
            value_pair = jnp.concatenate(
                [
                    jnp.concatenate([values * low, low], axis=1),
                    jnp.concatenate([values * high, high], axis=1),
                ],
                axis=0,
            )
            acc[slab] += jnp.dot(weights, value_pair, preferred_element_type=jnp.float32)

    def visit(first, second, peer):
        wanted = jnp.float32(0.0)
        tally = []
        for mine in range(2):
            total = None
            for slot in range(slots):
                name = block_ref[mine, slot]
                hit = jnp.logical_and(lax.div(name, 2) == peer, slot < live_ref[mine])
                factor = jnp.where(hit, 1.0, 0.0).astype(jnp.float32)
                wanted = jnp.maximum(wanted, factor * lax.rem(name, 2).astype(jnp.float32))
                term = counts[mine * slots + slot] * factor
                total = term if total is None else total + term
            tally.append(total)
        picked = first.astype(jnp.float32) * (1.0 - wanted) + second.astype(jnp.float32) * wanted
        normed = normalize(picked, gain)
        kv = jnp.dot(normed, w_in[:, width:], preferred_element_type=jnp.float32)
        attend(kv.astype(jnp.bfloat16), jnp.concatenate(tally, axis=0))

    def visit_pair(base, hops):
        def one(side, carry):
            far = (chip + 2 * chips + (2 * side - 1) * hops) % chips
            other = (core + base // 2) % 2
            visit(ring[base + side, 2 * hops - 2], ring[base + side, 2 * hops - 1], far * 2 + other)
            return carry

        lax.fori_loop(0, 2, one, 0)

    load_x.wait()
    load_in.wait()
    acc[...] = jnp.zeros_like(acc)
    for part in range(2):
        at = pl.ds(part * block, block)
        normed = normalize(x_own[at, :].astype(jnp.float32), gain)
        projected = jnp.dot(normed, w_in[...], preferred_element_type=jnp.float32)
        queries[at, :] = projected[:, :width].astype(jnp.bfloat16)
        own_kv[at, :] = projected[:, width:].astype(jnp.bfloat16)

    row_id = lax.broadcasted_iota(jnp.int32, (block, block), 0)

    def count(index_rows, edges):
        total = None
        for edge in range(edges):
            term = jnp.where(index_rows[edge : edge + 1, :] == row_id, 1.0, 0.0)
            total = term if total is None else total + term
        return total.T

    def count_slot(slot, carry):
        counts[slot] = count(rows_ref[slot], slot_edges)
        return carry

    lax.fori_loop(0, 2 * slots, count_slot, 0)
    for part in range(2):
        counts[2 * slots + part] = count(
            local_ref[:, part * block : (part + 1) * block], local_edges
        )

    arrived(0, 0)
    arrived(1, 0)
    for side in range(2):
        onward(side, ring.at[side, 0], 2).start()
        across(side, 0).start()

    vid_wide[...] = jnp.broadcast_to(vid_ref[...].astype(jnp.float32), (LANES, rows)).T
    low_rows = jnp.concatenate([low_f, low_f], axis=0)
    high_rows = jnp.concatenate([high_f, high_f], axis=0)
    members = [jnp.where(vid_wide[...] == float(j), 1.0, 0.0) for j in range(virtuals)]
    for slab in range(slabs):
        at = slab * LANES
        keys = own_kv[:, at : at + LANES].astype(jnp.float32)
        values = own_kv[:, width + at : width + at + LANES].astype(jnp.float32)
        own_key = None
        for j in range(virtuals):
            term = members[j] * vkey_ref[j : j + 1, at : at + LANES].astype(jnp.float32)
            own_key = term if own_key is None else own_key + term
        product = own_key * keys
        raw = low_rows * jnp.sum(product * low_rows, axis=1, keepdims=True)
        raw = raw + high_rows * jnp.sum(product * high_rows, axis=1, keepdims=True)
        weight = weight_of(raw, head_width).astype(jnp.bfloat16).astype(jnp.float32)
        weighted = weight * values
        for j in range(virtuals):
            pool[j : j + 1, at : at + LANES] = jnp.sum(weighted * members[j], axis=0, keepdims=True)
            pool[virtuals + j : virtuals + j + 1, at : at + LANES] = jnp.sum(
                weight * members[j], axis=0, keepdims=True
            )
    pool_sum[...] = pool[...]

    arrived(0, 1)
    arrived(1, 1)
    for side in range(2):
        onward(side, ring.at[side, 1], 3).start()
        across(side, 1).start()
        pool_onward(side, pool, 1).start()

    def local(part, carry):
        flag = part.astype(jnp.float32)
        tally = jnp.concatenate(
            [counts[2 * slots] * (1.0 - flag), counts[2 * slots + 1] * flag], axis=0
        )
        attend(own_kv[pl.ds(pl.multiple_of(part * block, block), block), :], tally)
        return carry

    lax.fori_loop(0, 2, local, 0)
    visit_pair(0, 1)

    def advance(step, carry):
        hops = step // 2 + 1
        pool_hops = step - (last - 1 - half)

        @pl.when(pool_hops >= 1)
        def _():
            for side in range(2):

                def take():
                    pool_onward(side, pool, pool_hops).wait_recv()
                    pool_sum[...] += pool_ring[side, pool_hops]

                if side == 0:
                    take()
                else:
                    pl.when(pool_hops < half)(take)
                limit = half if side == 0 else half - 1

                @pl.when(pool_hops < limit)
                def _():
                    pool_onward(side, pool_ring.at[side, pool_hops], pool_hops + 1).start()

        arrived(0, step)
        arrived(1, step)

        @pl.when(step + 2 <= last)
        def _():
            onward(0, ring.at[0, step], step + 2).start()

        @pl.when(step + 2 < last)
        def _():
            onward(1, ring.at[1, step], step + 2).start()

        @pl.when(step + 1 == last)
        def _():
            onward(1, ring.at[1, last - 1], last).start()

        across(0, step).start()
        across(1, step).start()

        @pl.when(step % 2 == 0)
        def _():
            for side in range(2):
                arrived(2 + side, step - 2)
                arrived(2 + side, step - 1)

        def pair(side, inner):
            odd = step % 2
            base = 2 - 2 * odd
            back = hops - 1 + odd
            far = (chip + 2 * chips + (2 * side - 1) * back) % chips
            other = (core + 1 - odd) % 2
            visit(
                ring[base + side, 2 * back - 2],
                ring[base + side, 2 * back - 1],
                far * 2 + other,
            )
            return inner

        lax.fori_loop(0, 2, pair, 0)
        return carry

    lax.fori_loop(2, last, advance, 0)

    for side in range(2):
        arrived(2 + side, last - 2)
        arrived(2 + side, last - 1)
    visit_pair(2, half - 1)
    arrived(0, last)
    arrived(1, last)
    across(0, last).start()
    across(1, last).start()
    swap = remote(pool_sum, pool_near, pool_sem.at[0], pool_sem.at[1], {"node": partner})
    swap.start()
    own_out.wait_recv()
    visit(near[:block, :], near[block:, :], partner)
    far_chip = (chip + half) % chips

    visit(ring[0, last], ring[1, last], far_chip * 2 + core)
    arrived(2, last)
    arrived(3, last)
    visit(ring[2, last], ring[3, last], far_chip * 2 + (1 - core))
    swap.wait_recv()
    load_out.wait()

    whole = pool_sum[...] + pool_near[...]
    pooled = whole[:virtuals] / whole[virtuals : 2 * virtuals]
    pieces = 4
    piece = rows // pieces

    def handoff(index):
        at = pl.ds(index * piece, piece)
        return remote(
            stage.at[at],
            out_hbm.at[at],
            out_send.at[index],
            out_recv.at[index],
            {"segment": following},
        )

    for index in range(pieces):
        at = slice(index * piece, (index + 1) * piece)
        mixed = []
        for slab in range(slabs):
            cols = slice(slab * LANES, (slab + 1) * LANES)
            attended = acc[slab, at, :LANES] / acc[slab, at, LANES:]
            for j in range(virtuals):
                mask = jnp.where(vid_wide[at, :] == float(j), 1.0, 0.0)
                attended = attended + mask * pooled[j : j + 1, cols]
            mixed.append(attended.astype(jnp.bfloat16))
        update = jnp.dot(
            jnp.concatenate(mixed, axis=1), w_out[...], preferred_element_type=jnp.float32
        )
        stage[at, :] = (x_own[at, :].astype(jnp.float32) + update).astype(jnp.bfloat16)
        if index:
            handoff(index - 1).start()
    handoff(pieces - 1).start()

    def drain_main(at, carry):
        for side in range(2):
            onward(side, ring.at[side, at], at).wait_send()
            across(side, at).wait_send()
        return carry

    lax.fori_loop(0, chunks, drain_main, 0)

    def drain_pool(at, carry):
        pool_onward(0, pool, at).wait_send()
        return carry

    lax.fori_loop(1, half + 1, drain_pool, 0)

    def drain_pool_left(at, carry):
        pool_onward(1, pool, at).wait_send()
        return carry

    lax.fori_loop(1, half, drain_pool_left, 0)
    own_out.wait_send()
    swap.wait_send()
    for index in range(pieces):
        handoff(index).wait()


def body(
    activations,
    norm_gain,
    project_in,
    project_out,
    virtual_keys,
    virtual_id,
    local_rows,
    slot_block,
    slot_count,
    slot_rows,
):
    rows, width = activations.shape[1:]
    block = slot_rows.shape[3]
    slots, slot_edges = slot_rows.shape[1:3]
    local_edges = local_rows.shape[0]
    virtuals = virtual_keys.shape[1]
    chips = lax.axis_size("node") // 2
    sections = lax.axis_size("segment")
    half = chips // 2
    chunks = chips - 1
    slabs = width // LANES
    sizes = (chips, sections, block, width, slots, slot_edges, local_edges, virtuals)
    vmem = pl.BlockSpec(memory_space=pltpu.VMEM)
    smem = pl.BlockSpec(memory_space=pltpu.SMEM)
    anywhere = pl.BlockSpec(memory_space=pl.ANY)
    bf16 = jnp.bfloat16
    f32 = jnp.float32
    out = pl.pallas_call(
        functools.partial(layer_kernel, sizes),
        out_shape=jax.ShapeDtypeStruct((rows, width), bf16),
        in_specs=[anywhere, vmem, anywhere, anywhere, vmem, vmem, vmem, smem, smem, vmem],
        out_specs=anywhere,
        scratch_shapes=[
            pltpu.VMEM((rows, width), bf16),
            pltpu.VMEM((width, 3 * width), bf16),
            pltpu.VMEM((width, width), bf16),
            pltpu.VMEM((rows, width), bf16),
            pltpu.VMEM((rows, 2 * width), bf16),
            pltpu.VMEM((4, chunks, block, width), bf16),
            pltpu.VMEM((rows, width), bf16),
            pltpu.VMEM((2 * slots + 2, block, block), f32),
            pltpu.VMEM((slabs, rows, 2 * LANES), f32),
            pltpu.VMEM((rows, LANES), f32),
            pltpu.VMEM((2 * virtuals, width), f32),
            pltpu.VMEM((2, half + 1, 2 * virtuals, width), f32),
            pltpu.VMEM((2 * virtuals, width), f32),
            pltpu.VMEM((2 * virtuals, width), f32),
            pltpu.VMEM((rows, width), bf16),
            pltpu.SemaphoreType.DMA((3,)),
            pltpu.SemaphoreType.DMA((2, chunks)),
            pltpu.SemaphoreType.DMA((2, chunks)),
            pltpu.SemaphoreType.DMA((4, chunks)),
            pltpu.SemaphoreType.DMA((2,)),
            pltpu.SemaphoreType.DMA((2, half + 1)),
            pltpu.SemaphoreType.DMA((2, half + 1)),
            pltpu.SemaphoreType.DMA((2,)),
            pltpu.SemaphoreType.DMA((4,)),
            pltpu.SemaphoreType.DMA((4,)),
        ],
        compiler_params=pltpu.CompilerParams(collective_id=0, has_side_effects=True),
        name="layer",
    )(
        activations[0],
        norm_gain,
        project_in[0],
        project_out[0],
        virtual_keys[0],
        virtual_id.reshape(1, rows),
        local_rows,
        slot_block,
        slot_count,
        slot_rows.reshape(-1, slot_edges, block),
    )
    return out[None]


def solution(mesh):
    placed = (
        P("segment", "node", None),
        P("segment", None),
        P("segment", None, None),
        P("segment", None, None),
        P("segment", None, None),
        P("node", None),
        P(None, "node"),
        P("node", None),
        P("node"),
        P("node", None, None, None),
    )
    return jax.shard_map(
        body, mesh=mesh, in_specs=placed, out_specs=P("segment", "node", None), check_vma=False
    )
```

```python
import functools
import math

import jax
import jax.numpy as jnp
from jax import lax
from jax.experimental import pallas as pl
from jax.experimental.pallas import tpu as pltpu
from jax.sharding import PartitionSpec as P

HEADS = 8
LANES = 128
CAP = 10.0
EPSILON = 1e-05
MESH = pl.DeviceIdType.MESH


def normalize(wide, gain):
    center = wide - jnp.mean(wide, axis=-1, keepdims=True)
    spread = jnp.mean(center * center, axis=-1, keepdims=True)
    return (center * lax.rsqrt(spread + EPSILON) * gain).astype(jnp.bfloat16)


def weight_of(raw, head_width):
    inner = jnp.tanh(raw * (head_width**-0.5 / CAP))
    return jnp.exp2(inner * (CAP * math.log2(math.e)))


def layer_kernel(
    sizes,
    x_hbm,
    gain_hbm,
    win_hbm,
    wout_hbm,
    vkey_hbm,
    vid_hbm,
    local_hbm,
    block_hbm,
    live_hbm,
    rows_hbm,
    out_hbm,
    gain_ref,
    vkey_ref,
    vid_ref,
    local_ref,
    block_ref,
    live_ref,
    rows_ref,
    x_own,
    w_in,
    w_out,
    queries,
    own_kv,
    ring,
    near,
    counts,
    acc,
    vid_wide,
    pool_sum,
    pool_out,
    pool_far,
    pool_near,
    stage,
    load_sem,
    main_send,
    near_send,
    ring_recv,
    own_sem,
    pool_send,
    pool_recv,
    pool_sem,
    out_send,
    out_recv,
):
    chips, sections, block, width, slots, slot_edges, local_edges, virtuals = sizes
    rows = 2 * block
    head_width = width // HEADS
    slabs = width // LANES
    half = chips // 2
    chunks = chips - 1
    last = chunks - 1
    me = lax.axis_index("node")
    section = lax.axis_index("segment")
    chip = me // 2
    core = me % 2
    right = (me + 2) % (2 * chips)
    left = (me + 2 * chips - 2) % (2 * chips)
    partner = chip * 2 + (1 - core)
    shifts = (1, 2, 4, 4, 4)
    marks = (4, 7, 10, 12)
    turns = len(shifts)
    assert chips == 16
    following = (section + 1) % sections
    previous = (section + sections - 1) % sections

    def remote(source, target, send, recv, device):
        return pltpu.make_async_remote_copy(
            src_ref=source,
            dst_ref=target,
            send_sem=send,
            recv_sem=recv,
            device_id=device,
            device_id_type=MESH,
        )

    beside = ({"node": right}, {"node": left})

    def onward(side, source, to):
        return remote(
            source, ring.at[side, to], main_send.at[side, to], ring_recv.at[side, to], beside[side]
        )

    def across(side, at):
        return remote(
            ring.at[side, at],
            ring.at[2 + side, at],
            near_send.at[side, at],
            ring_recv.at[2 + side, at],
            {"node": partner},
        )

    def arrived(lane, at):
        remote(
            ring.at[lane, at],
            ring.at[lane, at],
            near_send.at[0, 0],
            ring_recv.at[lane, at],
            {"node": partner},
        ).wait_recv()

    def pool_onward(turn):
        target = (me + 2 * chips + (1 - 2 * core) * 2 * shifts[turn]) % (2 * chips)
        return remote(
            pool_out.at[turn] if turn < 3 else pool_far.at[turn - 1],
            pool_far.at[turn],
            pool_send.at[turn],
            pool_recv.at[turn],
            {"node": target},
        )

    def pool_take(turn):
        pool_onward(turn).wait_recv()
        if 2 <= turn < turns - 1:
            pool_onward(turn + 1).start()
        total = pool_sum[...] + pool_far[turn].astype(jnp.float32)
        pool_sum[...] = total
        if turn < 2:
            pool_out[turn + 1] = total.astype(jnp.bfloat16)

    barrier = pltpu.get_barrier_semaphore()
    for device in (
        {"node": right},
        {"node": left},
        {"node": partner},
        {"segment": following},
        {"segment": previous},
    ):
        pl.semaphore_signal(barrier, inc=1, device_id=device, device_id_type=MESH)
    pl.semaphore_wait(barrier, 5)

    for part in range(2):
        for side in range(2):
            onward(side, x_hbm.at[pl.ds(part * block, block)], part).start()
    own_out = remote(x_hbm, near, own_sem.at[0], own_sem.at[1], {"node": partner})
    own_out.start()
    moves = (
        (x_hbm, x_own),
        (gain_hbm, gain_ref),
        (win_hbm, w_in),
        (rows_hbm, rows_ref),
        (local_hbm, local_ref),
        (vid_hbm, vid_ref),
        (vkey_hbm, vkey_ref),
        (block_hbm, block_ref),
        (live_hbm, live_ref),
        (wout_hbm, w_out),
    )
    loads = [
        pltpu.make_async_copy(source, target, load_sem.at[index])
        for index, (source, target) in enumerate(moves)
    ]
    for load in loads:
        load.start()

    lane = lax.broadcasted_iota(jnp.int32, (block, LANES), 1)
    low_f = jnp.where(lane < head_width, 1.0, 0.0).astype(jnp.float32)
    high_f = 1.0 - low_f
    low = low_f.astype(jnp.bfloat16)
    high = high_f.astype(jnp.bfloat16)

    def attend(kv, tally):
        doubled = jnp.concatenate([tally, tally], axis=1)
        for slab in range(slabs):
            at = slab * LANES
            keys = kv[:, at : at + LANES]
            values = kv[:, width + at : width + at + LANES]
            key_pair = jnp.concatenate([keys * low, keys * high], axis=0)
            raw = lax.dot_general(
                queries[:, at : at + LANES],
                key_pair,
                (((1,), (1,)), ((), ())),
                preferred_element_type=jnp.float32,
            )
            weights = (doubled * weight_of(raw, head_width)).astype(jnp.bfloat16)
            value_pair = jnp.concatenate(
                [
                    jnp.concatenate([values * low, low], axis=1),
                    jnp.concatenate([values * high, high], axis=1),
                ],
                axis=0,
            )
            acc[slab] += jnp.dot(weights, value_pair, preferred_element_type=jnp.float32)

    def visit(first, second, peer):
        wanted = jnp.float32(0.0)
        tally = []
        for mine in range(2):
            total = None
            for slot in range(slots):
                name = block_ref[mine, slot]
                hit = jnp.logical_and(lax.div(name, 2) == peer, slot < live_ref[mine])
                factor = jnp.where(hit, 1.0, 0.0).astype(jnp.float32)
                wanted = jnp.maximum(wanted, factor * lax.rem(name, 2).astype(jnp.float32))
                term = counts[mine * slots + slot] * factor
                total = term if total is None else total + term
            tally.append(total)
        picked = first.astype(jnp.float32) * (1.0 - wanted) + second.astype(jnp.float32) * wanted
        normed = normalize(picked, gain_ref[...])
        kv = jnp.dot(normed, w_in[:, width:], preferred_element_type=jnp.float32)
        attend(kv.astype(jnp.bfloat16), jnp.concatenate(tally, axis=0))

    def visit_pair(base, hops):
        def one(side, carry):
            far = (chip + 2 * chips + (2 * side - 1) * hops) % chips
            other = (core + base // 2) % 2
            visit(ring[base + side, 2 * hops - 2], ring[base + side, 2 * hops - 1], far * 2 + other)
            return carry

        lax.fori_loop(0, 2, one, 0)

    for load in loads[:3]:
        load.wait()
    acc[...] = jnp.zeros_like(acc)
    for part in range(2):
        at = pl.ds(part * block, block)
        normed = normalize(x_own[at, :].astype(jnp.float32), gain_ref[...])
        projected = jnp.dot(normed, w_in[...], preferred_element_type=jnp.float32)
        queries[at, :] = projected[:, :width].astype(jnp.bfloat16)
        own_kv[at, :] = projected[:, width:].astype(jnp.bfloat16)

    for load in loads[3:]:
        load.wait()

    row_id = lax.broadcasted_iota(jnp.int32, (block, block), 0)

    def count(index_rows, edges):
        total = None
        for edge in range(edges):
            term = jnp.where(index_rows[edge : edge + 1, :] == row_id, 1.0, 0.0)
            total = term if total is None else total + term
        return total.T

    def count_slot(slot, carry):
        counts[slot] = count(rows_ref[slot], slot_edges)
        return carry

    lax.fori_loop(0, 2 * slots, count_slot, 0)
    for part in range(2):
        counts[2 * slots + part] = count(
            local_ref[:, part * block : (part + 1) * block], local_edges
        )

    for side in range(2):
        arrived(side, 0)
        onward(side, ring.at[side, 0], 2).start()
        across(side, 0).start()

    vid_wide[...] = jnp.broadcast_to(vid_ref[...].astype(jnp.float32), (LANES, rows)).T
    low_rows = jnp.concatenate([low_f, low_f], axis=0)
    high_rows = jnp.concatenate([high_f, high_f], axis=0)
    packed = [None] * virtuals
    members = [jnp.where(vid_wide[...] == float(j), 1.0, 0.0) for j in range(virtuals)]
    for slab in range(slabs):
        at = slab * LANES
        keys = own_kv[:, at : at + LANES].astype(jnp.float32)
        values = own_kv[:, width + at : width + at + LANES].astype(jnp.float32)
        own_key = None
        for j in range(virtuals):
            term = members[j] * vkey_ref[j : j + 1, at : at + LANES].astype(jnp.float32)
            own_key = term if own_key is None else own_key + term
        product = own_key * keys
        raw = low_rows * jnp.sum(product * low_rows, axis=1, keepdims=True)
        raw = raw + high_rows * jnp.sum(product * high_rows, axis=1, keepdims=True)
        weight = weight_of(raw, head_width).astype(jnp.bfloat16).astype(jnp.float32)
        weighted = weight * values
        tag = jnp.where(lane[:1] % head_width == slab, 1.0, 0.0)
        for j in range(virtuals):
            pool_sum[j : j + 1, at : at + LANES] = jnp.sum(
                weighted * members[j], axis=0, keepdims=True
            )
            total = jnp.sum(weight * members[j], axis=0, keepdims=True) * tag
            packed[j] = total if packed[j] is None else packed[j] + total
    for j in range(virtuals):
        pool_sum[j : j + 1, width:] = packed[j]
    pool_out[0] = pool_sum[...].astype(jnp.bfloat16)

    for side in range(2):
        arrived(side, 1)
        onward(side, ring.at[side, 1], 3).start()
        across(side, 1).start()

    def local(part, carry):
        flag = part.astype(jnp.float32)
        tally = jnp.concatenate(
            [counts[2 * slots] * (1.0 - flag), counts[2 * slots + 1] * flag], axis=0
        )
        attend(own_kv[pl.ds(pl.multiple_of(part * block, block), block), :], tally)
        return carry

    pool_onward(0).start()
    lax.fori_loop(0, 2, local, 0)
    visit_pair(0, 1)

    def advance(step, carry):
        hops = step // 2 + 1

        for turn, mark in enumerate(marks):
            pl.when(step == mark)(functools.partial(pool_take, turn))

        arrived(0, step)

        @pl.when(step + 2 <= last)
        def _():
            onward(0, ring.at[0, step], step + 2).start()

        across(0, step).start()
        arrived(1, step)

        @pl.when(step + 2 < last)
        def _():
            onward(1, ring.at[1, step], step + 2).start()

        @pl.when(step + 1 == last)
        def _():
            onward(1, ring.at[1, last - 1], last).start()

        across(1, step).start()

        @pl.when(step % 2 == 0)
        def _():
            for side in range(2):
                arrived(2 + side, step - 2)
                arrived(2 + side, step - 1)

        def pair(side, inner):
            odd = step % 2
            base = 2 - 2 * odd
            back = hops - 1 + odd
            far = (chip + 2 * chips + (2 * side - 1) * back) % chips
            other = (core + 1 - odd) % 2
            visit(
                ring[base + side, 2 * back - 2],
                ring[base + side, 2 * back - 1],
                far * 2 + other,
            )
            return inner

        lax.fori_loop(0, 2, pair, 0)
        for turn in (1, 2):

            @pl.when(step == marks[turn - 1])
            def _():
                pool_onward(turn).start()

        return carry

    lax.fori_loop(2, last, advance, 0)

    for side in range(2):
        arrived(2 + side, last - 2)
        arrived(2 + side, last - 1)
    visit_pair(2, half - 1)
    pool_take(turns - 1)
    arrived(0, last)
    arrived(1, last)
    across(0, last).start()
    across(1, last).start()
    own_out.wait_recv()
    visit(near[:block, :], near[block:, :], partner)
    swap = remote(pool_sum, pool_near, pool_sem.at[0], pool_sem.at[1], {"node": partner})
    swap.start()
    far_chip = (chip + half) % chips

    visit(ring[0, last], ring[1, last], far_chip * 2 + core)
    arrived(2, last)
    arrived(3, last)
    visit(ring[2, last], ring[3, last], far_chip * 2 + (1 - core))
    swap.wait_recv()

    whole = pool_sum[...] + pool_near[...]
    pooled = []
    spot = lane[:virtuals]
    for slab in range(slabs):
        totals = whole[:, width:]
        below = jnp.sum(jnp.where(spot == slab, totals, 0.0), axis=1, keepdims=True)
        above = jnp.sum(jnp.where(spot == head_width + slab, totals, 0.0), axis=1, keepdims=True)
        pooled.append(
            whole[:, slab * LANES : (slab + 1) * LANES]
            / jnp.where(spot < head_width, below, above)
        )
    pieces = 4
    piece = rows // pieces

    def handoff(index):
        at = pl.ds(index * piece, piece)
        return remote(
            stage.at[at],
            out_hbm.at[at],
            out_send.at[index],
            out_recv.at[index],
            {"segment": following},
        )

    for index in range(pieces):
        at = slice(index * piece, (index + 1) * piece)
        mixed = []
        for slab in range(slabs):
            attended = acc[slab, at, :LANES] / acc[slab, at, LANES:]
            for j in range(virtuals):
                mask = jnp.where(vid_wide[at, :] == float(j), 1.0, 0.0)
                attended = attended + mask * pooled[slab][j : j + 1]
            mixed.append(attended.astype(jnp.bfloat16))
        update = jnp.dot(
            jnp.concatenate(mixed, axis=1), w_out[...], preferred_element_type=jnp.float32
        )
        stage[at, :] = (x_own[at, :].astype(jnp.float32) + update).astype(jnp.bfloat16)
        if index:
            handoff(index - 1).start()
    handoff(pieces - 1).start()

    def drain_main(at, carry):
        for side in range(2):
            onward(side, ring.at[side, at], at).wait_send()
            across(side, at).wait_send()
        return carry

    lax.fori_loop(0, chunks, drain_main, 0)

    for turn in range(turns):
        pool_onward(turn).wait_send()
    own_out.wait_send()
    swap.wait_send()
    for index in range(pieces):
        handoff(index).wait()


def body(
    activations,
    norm_gain,
    project_in,
    project_out,
    virtual_keys,
    virtual_id,
    local_rows,
    slot_block,
    slot_count,
    slot_rows,
):
    rows, width = activations.shape[1:]
    block = slot_rows.shape[3]
    slots, slot_edges = slot_rows.shape[1:3]
    local_edges = local_rows.shape[0]
    virtuals = virtual_keys.shape[1]
    chips = lax.axis_size("node") // 2
    sections = lax.axis_size("segment")
    chunks = chips - 1
    slabs = width // LANES
    sizes = (chips, sections, block, width, slots, slot_edges, local_edges, virtuals)
    vmem = pl.BlockSpec(memory_space=pltpu.VMEM)
    anywhere = pl.BlockSpec(memory_space=pl.ANY)
    bf16 = jnp.bfloat16
    f32 = jnp.float32
    out = pl.pallas_call(
        functools.partial(layer_kernel, sizes),
        out_shape=pltpu.VMEM((rows, width), bf16),
        in_specs=[anywhere] * 10,
        out_specs=vmem,
        scratch_shapes=[
            pltpu.VMEM((1, width), f32),
            pltpu.VMEM((virtuals, width), bf16),
            pltpu.VMEM((1, rows), jnp.int32),
            pltpu.VMEM((local_edges, rows), jnp.int32),
            pltpu.SMEM((2, slots), jnp.int32),
            pltpu.SMEM((2,), jnp.int32),
            pltpu.VMEM((2 * slots, slot_edges, block), jnp.int32),
            pltpu.VMEM((rows, width), bf16),
            pltpu.VMEM((width, 3 * width), bf16),
            pltpu.VMEM((width, width), bf16),
            pltpu.VMEM((rows, width), bf16),
            pltpu.VMEM((rows, 2 * width), bf16),
            pltpu.VMEM((4, chunks, block, width), bf16),
            pltpu.VMEM((rows, width), bf16),
            pltpu.VMEM((2 * slots + 2, block, block), f32),
            pltpu.VMEM((slabs, rows, 2 * LANES), f32),
            pltpu.VMEM((rows, LANES), f32),
            pltpu.VMEM((virtuals, width + LANES), f32),
            pltpu.VMEM((3, virtuals, width + LANES), bf16),
            pltpu.VMEM((5, virtuals, width + LANES), bf16),
            pltpu.VMEM((virtuals, width + LANES), f32),
            pltpu.VMEM((rows, width), bf16),
            pltpu.SemaphoreType.DMA((10,)),
            pltpu.SemaphoreType.DMA((2, chunks)),
            pltpu.SemaphoreType.DMA((2, chunks)),
            pltpu.SemaphoreType.DMA((4, chunks)),
            pltpu.SemaphoreType.DMA((2,)),
            pltpu.SemaphoreType.DMA((5,)),
            pltpu.SemaphoreType.DMA((5,)),
            pltpu.SemaphoreType.DMA((2,)),
            pltpu.SemaphoreType.DMA((4,)),
            pltpu.SemaphoreType.DMA((4,)),
        ],
        compiler_params=pltpu.CompilerParams(collective_id=0, has_side_effects=True),
        name="layer",
    )(
        activations[0],
        norm_gain,
        project_in[0],
        project_out[0],
        virtual_keys[0],
        virtual_id.reshape(1, rows),
        local_rows,
        slot_block,
        slot_count,
        slot_rows.reshape(-1, slot_edges, block),
    )
    return out[None]


def solution(mesh):
    placed = (
        P("segment", "node", None),
        P("segment", None),
        P("segment", None, None),
        P("segment", None, None),
        P("segment", None, None),
        P("node", None),
        P(None, "node"),
        P("node", None),
        P("node"),
        P("node", None, None, None),
    )
    return jax.shard_map(
        body, mesh=mesh, in_specs=placed, out_specs=P("segment", "node", None), check_vma=False
    )
```

```python
import functools
import math

import jax
import jax.numpy as jnp
from jax import lax
from jax.experimental import pallas as pl
from jax.experimental.pallas import tpu as pltpu
from jax.sharding import PartitionSpec as P

HEADS = 8
LANES = 128
CAP = 10.0
EPSILON = 1e-05
MESH = pl.DeviceIdType.MESH


def normalize(wide, gain):
    center = wide - jnp.mean(wide, axis=-1, keepdims=True)
    spread = jnp.mean(center * center, axis=-1, keepdims=True)
    return (center * lax.rsqrt(spread + EPSILON) * gain).astype(jnp.bfloat16)


def weight_of(raw, head_width):
    inner = jnp.tanh(raw * (head_width**-0.5 / CAP))
    return jnp.exp2(inner * (CAP * math.log2(math.e)))


def layer_kernel(
    sizes,
    x_hbm,
    gain_hbm,
    win_hbm,
    wout_hbm,
    vkey_hbm,
    vid_hbm,
    local_hbm,
    block_hbm,
    live_hbm,
    rows_hbm,
    out_hbm,
    gain_ref,
    vkey_ref,
    vid_ref,
    local_ref,
    block_ref,
    live_ref,
    rows_ref,
    x_own,
    w_in,
    w_out,
    queries,
    own_kv,
    ring,
    counts,
    acc,
    vid_wide,
    pool_sum,
    pool_out,
    pool_far,
    pool_near,
    stage,
    load_sem,
    main_send,
    near_send,
    ring_recv,
    own_sem,
    pool_send,
    pool_recv,
    pool_sem,
    out_send,
    out_recv,
):
    chips, sections, block, width, slots, slot_edges, local_edges, virtuals = sizes
    rows = 2 * block
    head_width = width // HEADS
    slabs = width // LANES
    half = chips // 2
    chunks = chips - 1
    last = chunks - 1
    me = lax.axis_index("node")
    section = lax.axis_index("segment")
    chip = me // 2
    core = me % 2
    right = (me + 2) % (2 * chips)
    left = (me + 2 * chips - 2) % (2 * chips)
    partner = chip * 2 + (1 - core)
    shifts = (1, 2, 4, 4, 4)
    marks = (4, 7, 10, 12)
    turns = len(shifts)
    assert chips == 16
    following = (section + 1) % sections
    previous = (section + sections - 1) % sections

    def remote(source, target, send, recv, device):
        return pltpu.make_async_remote_copy(
            src_ref=source,
            dst_ref=target,
            send_sem=send,
            recv_sem=recv,
            device_id=device,
            device_id_type=MESH,
        )

    beside = ({"node": right}, {"node": left})

    def onward(side, source, to):
        return remote(
            source, ring.at[side, to], main_send.at[side, to], ring_recv.at[side, to], beside[side]
        )

    def across(side, at):
        return remote(
            ring.at[side, at],
            ring.at[2 + side, at],
            near_send.at[side, at],
            ring_recv.at[2 + side, at],
            {"node": partner},
        )

    def arrived(lane, at):
        remote(
            ring.at[lane, at],
            ring.at[lane, at],
            near_send.at[0, 0],
            ring_recv.at[lane, at],
            {"node": partner},
        ).wait_recv()

    def pool_onward(turn):
        target = (me + 2 * chips + (1 - 2 * core) * 2 * shifts[turn]) % (2 * chips)
        return remote(
            pool_out.at[turn] if turn < 3 else pool_far.at[turn - 1],
            pool_far.at[turn],
            pool_send.at[turn],
            pool_recv.at[turn],
            {"node": target},
        )

    def pool_take(turn):
        pool_onward(turn).wait_recv()
        if 2 <= turn < turns - 1:
            pool_onward(turn + 1).start()
        total = pool_sum[...] + pool_far[turn].astype(jnp.float32)
        pool_sum[...] = total
        if turn < 2:
            pool_out[turn + 1] = total.astype(jnp.bfloat16)

    barrier = pltpu.get_barrier_semaphore()
    for device in (
        {"node": right},
        {"node": left},
        {"node": partner},
        {"segment": following},
        {"segment": previous},
    ):
        pl.semaphore_signal(barrier, inc=1, device_id=device, device_id_type=MESH)
    pl.semaphore_wait(barrier, 5)

    for part in range(2):
        for side in range(2):
            onward(side, x_hbm.at[pl.ds(part * block, block)], part).start()
    own_out = [
        remote(
            x_hbm.at[pl.ds(part * block, block)],
            ring.at[4, part],
            own_sem.at[part],
            own_sem.at[2 + part],
            {"node": partner},
        )
        for part in range(2)
    ]
    for copy in own_out:
        copy.start()
    moves = (
        (x_hbm, x_own),
        (gain_hbm, gain_ref),
        (win_hbm, w_in),
        (rows_hbm, rows_ref),
        (local_hbm, local_ref),
        (vid_hbm, vid_ref),
        (vkey_hbm, vkey_ref),
        (block_hbm, block_ref),
        (live_hbm, live_ref),
        (wout_hbm, w_out),
    )
    loads = [
        pltpu.make_async_copy(source, target, load_sem.at[index])
        for index, (source, target) in enumerate(moves)
    ]
    for load in loads:
        load.start()

    lane = lax.broadcasted_iota(jnp.int32, (block, LANES), 1)
    low_f = jnp.where(lane < head_width, 1.0, 0.0).astype(jnp.float32)
    high_f = 1.0 - low_f
    low = low_f.astype(jnp.bfloat16)
    high = high_f.astype(jnp.bfloat16)

    def attend(kv, tally):
        doubled = jnp.concatenate([tally, tally], axis=1)
        for slab in range(slabs):
            at = slab * LANES
            keys = kv[:, at : at + LANES]
            values = kv[:, width + at : width + at + LANES]
            key_pair = jnp.concatenate([keys * low, keys * high], axis=0)
            raw = lax.dot_general(
                queries[:, at : at + LANES],
                key_pair,
                (((1,), (1,)), ((), ())),
                preferred_element_type=jnp.float32,
            )
            weights = (doubled * weight_of(raw, head_width)).astype(jnp.bfloat16)
            value_pair = jnp.concatenate(
                [
                    jnp.concatenate([values * low, low], axis=1),
                    jnp.concatenate([values * high, high], axis=1),
                ],
                axis=0,
            )
            acc[slab] += jnp.dot(weights, value_pair, preferred_element_type=jnp.float32)

    def visit(first, second, peer):
        wanted = jnp.float32(0.0)
        tally = []
        for mine in range(2):
            total = None
            for slot in range(slots):
                name = block_ref[mine, slot]
                hit = jnp.logical_and(lax.div(name, 2) == peer, slot < live_ref[mine])
                factor = jnp.where(hit, 1.0, 0.0).astype(jnp.float32)
                wanted = jnp.maximum(wanted, factor * lax.rem(name, 2).astype(jnp.float32))
                term = counts[mine * slots + slot] * factor
                total = term if total is None else total + term
            tally.append(total)
        picked = first.astype(jnp.float32) * (1.0 - wanted) + second.astype(jnp.float32) * wanted
        normed = normalize(picked, gain_ref[...])
        kv = jnp.dot(normed, w_in[:, width:], preferred_element_type=jnp.float32)
        attend(kv.astype(jnp.bfloat16), jnp.concatenate(tally, axis=0))

    def visit_pair(base, hops):
        def one(side, carry):
            far = (chip + 2 * chips + (2 * side - 1) * hops) % chips
            other = (core + base // 2) % 2
            visit(ring[base + side, 2 * hops - 2], ring[base + side, 2 * hops - 1], far * 2 + other)
            return carry

        lax.fori_loop(0, 2, one, 0)

    for load in loads[:3]:
        load.wait()
    acc[...] = jnp.zeros_like(acc)
    for part in range(2):
        at = pl.ds(part * block, block)
        normed = normalize(x_own[at, :].astype(jnp.float32), gain_ref[...])
        projected = jnp.dot(normed, w_in[...], preferred_element_type=jnp.float32)
        queries[at, :] = projected[:, :width].astype(jnp.bfloat16)
        own_kv[at, :] = projected[:, width:].astype(jnp.bfloat16)

    for load in loads[3:]:
        load.wait()

    row_id = lax.broadcasted_iota(jnp.int32, (block, block), 0)

    def count(index_rows, edges):
        total = None
        for edge in range(edges):
            term = jnp.where(index_rows[edge : edge + 1, :] == row_id, 1.0, 0.0)
            total = term if total is None else total + term
        return total.T

    def count_slot(slot, carry):
        counts[slot] = count(rows_ref[slot], slot_edges)
        return carry

    lax.fori_loop(0, 2 * slots, count_slot, 0)
    for part in range(2):
        counts[2 * slots + part] = count(
            local_ref[:, part * block : (part + 1) * block], local_edges
        )

    for side in range(2):
        arrived(side, 0)
        onward(side, ring.at[side, 0], 2).start()
        across(side, 0).start()

    vid_wide[...] = jnp.broadcast_to(vid_ref[...].astype(jnp.float32), (LANES, rows)).T
    low_rows = jnp.concatenate([low_f, low_f], axis=0)
    high_rows = jnp.concatenate([high_f, high_f], axis=0)
    packed = [None] * virtuals
    members = [jnp.where(vid_wide[...] == float(j), 1.0, 0.0) for j in range(virtuals)]
    for slab in range(slabs):
        at = slab * LANES
        keys = own_kv[:, at : at + LANES].astype(jnp.float32)
        values = own_kv[:, width + at : width + at + LANES].astype(jnp.float32)
        own_key = None
        for j in range(virtuals):
            term = members[j] * vkey_ref[j : j + 1, at : at + LANES].astype(jnp.float32)
            own_key = term if own_key is None else own_key + term
        product = own_key * keys
        raw = low_rows * jnp.sum(product * low_rows, axis=1, keepdims=True)
        raw = raw + high_rows * jnp.sum(product * high_rows, axis=1, keepdims=True)
        weight = weight_of(raw, head_width).astype(jnp.bfloat16).astype(jnp.float32)
        weighted = weight * values
        tag = jnp.where(lane[:1] % head_width == slab, 1.0, 0.0)
        for j in range(virtuals):
            pool_sum[j : j + 1, at : at + LANES] = jnp.sum(
                weighted * members[j], axis=0, keepdims=True
            )
            total = jnp.sum(weight * members[j], axis=0, keepdims=True) * tag
            packed[j] = total if packed[j] is None else packed[j] + total
    for j in range(virtuals):
        pool_sum[j : j + 1, width:] = packed[j]
    pool_out[0] = pool_sum[...].astype(jnp.bfloat16)

    for side in range(2):
        arrived(side, 1)
        onward(side, ring.at[side, 1], 3).start()
        across(side, 1).start()

    def local(part, carry):
        flag = part.astype(jnp.float32)
        tally = jnp.concatenate(
            [counts[2 * slots] * (1.0 - flag), counts[2 * slots + 1] * flag], axis=0
        )
        attend(own_kv[pl.ds(pl.multiple_of(part * block, block), block), :], tally)
        return carry

    pool_onward(0).start()
    lax.fori_loop(0, 2, local, 0)
    visit_pair(0, 1)

    def advance(step, carry):
        hops = step // 2 + 1

        for turn, mark in enumerate(marks):
            pl.when(step == mark)(functools.partial(pool_take, turn))

        arrived(0, step)

        @pl.when(step + 2 <= last)
        def _():
            onward(0, ring.at[0, step], step + 2).start()

        across(0, step).start()
        arrived(1, step)

        @pl.when(step + 2 < last)
        def _():
            onward(1, ring.at[1, step], step + 2).start()

        @pl.when(step + 1 == last)
        def _():
            onward(1, ring.at[1, last - 1], last).start()

        across(1, step).start()

        @pl.when(step % 2 == 0)
        def _():
            for side in range(2):
                arrived(2 + side, step - 2)
                arrived(2 + side, step - 1)

        def pair(side, inner):
            odd = step % 2
            base = 2 - 2 * odd
            back = hops - 1 + odd
            far = (chip + 2 * chips + (2 * side - 1) * back) % chips
            other = (core + 1 - odd) % 2
            visit(
                ring[base + side, 2 * back - 2],
                ring[base + side, 2 * back - 1],
                far * 2 + other,
            )
            return inner

        lax.fori_loop(0, 2, pair, 0)
        for turn in (1, 2):

            @pl.when(step == marks[turn - 1])
            def _():
                pool_onward(turn).start()

        return carry

    lax.fori_loop(2, last, advance, 0)

    for side in range(2):
        arrived(2 + side, last - 2)
        arrived(2 + side, last - 1)
    visit_pair(2, half - 1)
    pool_take(turns - 1)
    arrived(0, last)
    arrived(1, last)
    across(0, last).start()
    across(1, last).start()
    for copy in own_out:
        copy.wait_recv()
    swap = remote(pool_sum, pool_near, pool_sem.at[0], pool_sem.at[1], {"node": partner})

    def finish(turn, carry):
        away = (turn + 1) // 2
        row = (2 * turn + 4) % 6

        @pl.when(turn == 1)
        def _():
            swap.start()

        @pl.when(turn == 2)
        def _():
            arrived(2, last)
            arrived(3, last)

        visit(
            ring[row, last * away],
            ring[row + away, 1 + (last - 1) * away],
            (chip + half * away) % chips * 2 + (core + 1 + turn) % 2,
        )
        return carry

    lax.fori_loop(0, 3, finish, 0)
    swap.wait_recv()

    whole = pool_sum[...] + pool_near[...]
    pooled = []
    spot = lane[:virtuals]
    for slab in range(slabs):
        totals = whole[:, width:]
        below = jnp.sum(jnp.where(spot == slab, totals, 0.0), axis=1, keepdims=True)
        above = jnp.sum(jnp.where(spot == head_width + slab, totals, 0.0), axis=1, keepdims=True)
        pooled.append(
            whole[:, slab * LANES : (slab + 1) * LANES]
            / jnp.where(spot < head_width, below, above)
        )
    pieces = 4
    piece = rows // pieces

    def handoff(index):
        at = pl.ds(index * piece, piece)
        return remote(
            stage.at[at],
            out_hbm.at[at],
            out_send.at[index],
            out_recv.at[index],
            {"segment": following},
        )

    for index in range(pieces):
        at = slice(index * piece, (index + 1) * piece)
        mixed = []
        for slab in range(slabs):
            attended = acc[slab, at, :LANES] / acc[slab, at, LANES:]
            for j in range(virtuals):
                mask = jnp.where(vid_wide[at, :] == float(j), 1.0, 0.0)
                attended = attended + mask * pooled[slab][j : j + 1]
            mixed.append(attended.astype(jnp.bfloat16))
        update = jnp.dot(
            jnp.concatenate(mixed, axis=1), w_out[...], preferred_element_type=jnp.float32
        )
        stage[at, :] = (x_own[at, :].astype(jnp.float32) + update).astype(jnp.bfloat16)
        if index:
            handoff(index - 1).start()
    handoff(pieces - 1).start()

    def drain_main(at, carry):
        for side in range(2):
            onward(side, ring.at[side, at], at).wait_send()
            across(side, at).wait_send()
        return carry

    lax.fori_loop(0, chunks, drain_main, 0)

    for turn in range(turns):
        pool_onward(turn).wait_send()
    for copy in own_out:
        copy.wait_send()
    swap.wait_send()
    for index in range(pieces):
        handoff(index).wait()


def body(
    activations,
    norm_gain,
    project_in,
    project_out,
    virtual_keys,
    virtual_id,
    local_rows,
    slot_block,
    slot_count,
    slot_rows,
):
    rows, width = activations.shape[1:]
    block = slot_rows.shape[3]
    slots, slot_edges = slot_rows.shape[1:3]
    local_edges = local_rows.shape[0]
    virtuals = virtual_keys.shape[1]
    chips = lax.axis_size("node") // 2
    sections = lax.axis_size("segment")
    chunks = chips - 1
    slabs = width // LANES
    sizes = (chips, sections, block, width, slots, slot_edges, local_edges, virtuals)
    vmem = pl.BlockSpec(memory_space=pltpu.VMEM)
    anywhere = pl.BlockSpec(memory_space=pl.ANY)
    bf16 = jnp.bfloat16
    f32 = jnp.float32
    out = pl.pallas_call(
        functools.partial(layer_kernel, sizes),
        out_shape=pltpu.VMEM((rows, width), bf16),
        in_specs=[anywhere] * 10,
        out_specs=vmem,
        scratch_shapes=[
            pltpu.VMEM((1, width), f32),
            pltpu.VMEM((virtuals, width), bf16),
            pltpu.VMEM((1, rows), jnp.int32),
            pltpu.VMEM((local_edges, rows), jnp.int32),
            pltpu.SMEM((2, slots), jnp.int32),
            pltpu.SMEM((2,), jnp.int32),
            pltpu.VMEM((2 * slots, slot_edges, block), jnp.int32),
            pltpu.VMEM((rows, width), bf16),
            pltpu.VMEM((width, 3 * width), bf16),
            pltpu.VMEM((width, width), bf16),
            pltpu.VMEM((rows, width), bf16),
            pltpu.VMEM((rows, 2 * width), bf16),
            pltpu.VMEM((5, chunks, block, width), bf16),
            pltpu.VMEM((2 * slots + 2, block, block), f32),
            pltpu.VMEM((slabs, rows, 2 * LANES), f32),
            pltpu.VMEM((rows, LANES), f32),
            pltpu.VMEM((virtuals, width + LANES), f32),
            pltpu.VMEM((3, virtuals, width + LANES), bf16),
            pltpu.VMEM((5, virtuals, width + LANES), bf16),
            pltpu.VMEM((virtuals, width + LANES), f32),
            pltpu.VMEM((rows, width), bf16),
            pltpu.SemaphoreType.DMA((10,)),
            pltpu.SemaphoreType.DMA((2, chunks)),
            pltpu.SemaphoreType.DMA((2, chunks)),
            pltpu.SemaphoreType.DMA((4, chunks)),
            pltpu.SemaphoreType.DMA((4,)),
            pltpu.SemaphoreType.DMA((5,)),
            pltpu.SemaphoreType.DMA((5,)),
            pltpu.SemaphoreType.DMA((2,)),
            pltpu.SemaphoreType.DMA((4,)),
            pltpu.SemaphoreType.DMA((4,)),
        ],
        compiler_params=pltpu.CompilerParams(collective_id=0, has_side_effects=True),
        name="layer",
    )(
        activations[0],
        norm_gain,
        project_in[0],
        project_out[0],
        virtual_keys[0],
        virtual_id.reshape(1, rows),
        local_rows,
        slot_block,
        slot_count,
        slot_rows.reshape(-1, slot_edges, block),
    )
    return out[None]


def solution(mesh):
    placed = (
        P("segment", "node", None),
        P("segment", None),
        P("segment", None, None),
        P("segment", None, None),
        P("segment", None, None),
        P("node", None),
        P(None, "node"),
        P("node", None),
        P("node"),
        P("node", None, None, None),
    )
    return jax.shard_map(
        body, mesh=mesh, in_specs=placed, out_specs=P("segment", "node", None), check_vma=False
    )
```
